32 devices in a mesh: gx: 4 (over x, core), gy: 8 (over z, y).
Axes of the slice: x: 2, y: 2, z: 4, core: 2. Of those that a mesh axis runs over, the one named last changes fastest.
Arguments:
- token_ids: int32 [192, 2], replicated, may hold values from 0 to 64127
- lengths: int32 [192], P(('gx', 'gy')), may hold values from 64 to 512, as said below
- embedding: bfloat16 [64128, 8192], P('gy', 'gx'), may hold values from -6 to 6
- norm_gain: float32 [8192], P('gx'), may hold values from 0.1 to 1.9
- qkv_weight: bfloat16 [8192, 10240], P('gx', 'gy'), may hold values from -0.0625 to 0.0625
- out_weight: bfloat16 [8192, 8192], P('gy', 'gx'), may hold values from -0.5 to 0.5
- key_cache: bfloat16 [192, 512, 1024], P(('gx', 'gy'))
- value_cache: bfloat16 [192, 512, 1024], P(('gx', 'gy')), may hold values from -6 to 6
Outputs:
- layer_out: bfloat16 [192, 2, 8192], P('gy', None, 'gx')
- new_keys: bfloat16 [192, 2, 1024], P(('gx', 'gy'))
- new_values: bfloat16 [192, 2, 1024], P(('gx', 'gy'))
The draws below stay inside these ranges and needn't reach their ends.
Inputs may be any that keep to these rules, and one draw needn't show every extreme that they name: `lengths`: every length is at least 64 and at most 512; some sequence has exactly 512.
All inputs are finite; a program needn't handle non-finite values.
Results may differ from the reference program's by a relative error of at most 0.012.
The reference program's roundings to bfloat16 on the way count: a program that leaves them out, or rounds other values in their place, can miss the bound.
Values may be sent and summed in bfloat16 or wider, within the bound.
No kernel may reach another device: no remote copies, remote signals or barrier semaphores. Data moves between devices by JAX's collectives and lax.ppermute only.
A program may use at most 192 MiB of HBM per device.

```python
import math
import jax
import jax.numpy as jnp
import numpy as np
from jax import lax

D = 8192
HEADS = 64
KV_HEADS = 8
HEAD_DIM = 128
VOCAB = 64128
SEQ_DEV = 6
CTX = 512
BATCH = 192
TOKENS = 384
QKV = 10240


def draw_lengths(key, part):
    first, second = jax.random.split(key)
    values = jax.random.randint(first, (BATCH,), CTX // 8, CTX + 1)
    spot = jax.random.randint(second, (), 0, BATCH)
    return jnp.where(jnp.arange(BATCH) == spot, CTX, values).astype(jnp.int32)


def draw_key_cache(key, part):
    first = jax.random.fold_in(jax.random.fold_in(key, 11), 0)
    width = KV_HEADS * HEAD_DIM
    base = jax.random.normal(first, (BATCH, CTX, width), dtype=jnp.float32)
    return base.astype(jnp.bfloat16)


def place_ends(entries, stream_key, smallest, high):
    dims = entries.shape
    index_at = [jax.random.randint(jax.random.fold_in(stream_key, axis), (), 0, dims[axis]) for axis in range(len(dims))]
    entries = entries.at[tuple(index_at)].set(smallest)
    longest = dims.index(max(dims))
    index_at[longest] = (index_at[longest] + 1) % dims[longest]
    return entries.at[tuple(index_at)].set(high)


def steps_of(own_key, dims, cuts, low, largest):
    level, own = 1.0, jax.random.fold_in(own_key, 6)
    for axis_at, blocks in cuts:
        steps = jnp.exp(jax.random.uniform(jax.random.fold_in(own, axis_at), (blocks,), jnp.float32, low / len(cuts), largest / len(cuts)))
        level = level * jnp.repeat(steps, dims[axis_at] // blocks).reshape([-1 if axis == axis_at else 1 for axis in range(len(dims))])
    return level


def rank_table(count, lean):
    loads = [(1 << 20) // math.isqrt(rank ** lean) + 1 for rank in range(1, count + 1)]
    spread = 1 + sum(loads) // (1 << 30)
    return np.cumsum(np.array([max(1, weight // spread) for weight in loads]))


def ranked(rng, dims, number_of, slope):
    table = rank_table(number_of, slope)
    lot = jax.random.randint(jax.random.fold_in(rng, 1), dims, 0, int(table[number_of - 1]))
    standing = jnp.searchsorted(jnp.asarray(table, jnp.int32), lot, side="right")
    return jax.random.permutation(jax.random.fold_in(rng, 2), number_of)[standing].astype(jnp.int32)


def centred(own_key, shape, deviation, limit, pieces=(), kind=jnp.bfloat16):
    level = steps_of(own_key, shape, pieces, -0.22, 0.18) if pieces else 1.0
    values = jax.random.normal(own_key, shape, jnp.float32) * deviation * level
    return jnp.minimum(jnp.maximum(values, -limit), limit).astype(kind)


def setup_inputs(seed: int = 0) -> dict:
    seeds = jax.random.split(jax.random.key(seed), 9)
    token_ids = place_ends(ranked(seeds[0], (BATCH, 2), VOCAB, 1), jax.random.fold_in(seeds[0], 3), 0, VOCAB - 1).astype(jnp.int32)
    lengths = draw_lengths(jax.random.fold_in(seeds[8], 71), 0)
    embedding = centred(seeds[2], (VOCAB, D), 1.0, 6.0, ((0, 8), (1, 4)))
    norm_gain = jnp.clip(1.0 + 0.18 * jax.random.normal(seeds[3], (D,), jnp.float32), 0.1, 1.9)
    qkv_weight = centred(seeds[4], (D, QKV), D ** -0.5, 0.0625, ((0, 4), (1, 8)))
    out_weight = centred(seeds[5], (D, D), (D // 64) ** -0.5, 0.5, ((0, 8), (1, 4)))
    key_cache = draw_key_cache(jax.random.fold_in(seeds[8], 71), 0)
    value_cache = centred(seeds[7], (BATCH, CTX, KV_HEADS * HEAD_DIM), 1.0, 6.0, ((0, 32),))
    return {"token_ids": token_ids, "lengths": lengths, "embedding": embedding, "norm_gain": norm_gain, "qkv_weight": qkv_weight, "out_weight": out_weight, "key_cache": key_cache, "value_cache": value_cache}


EPS = 1e-05

def rotate(values, positions):
    half = HEAD_DIM // 2
    freq = jnp.exp(-jnp.log(jnp.float32(500000.0)) * 2.0 * jnp.arange(half, dtype=jnp.float32) / HEAD_DIM)
    angle = positions[:, :, None, None] * freq[None, None, None, :]
    cosine = jnp.cos(angle)
    sine = jnp.sin(angle)
    lower = values[..., :half]
    upper = values[..., half:]
    return jnp.concatenate([lower * cosine - upper * sine, upper * cosine + lower * sine], axis=-1)

def attend_group(args):
    query, keys_new, vals_new, keys_old, vals_old, lens = args
    seqs = query.shape[0]
    group = HEADS // KV_HEADS
    scale = HEAD_DIM ** (-0.5)
    query_g = query.reshape(seqs, 2, KV_HEADS, group, HEAD_DIM)
    keys_c = keys_old.astype(jnp.float32).reshape(seqs, CTX, KV_HEADS, HEAD_DIM)
    vals_c = vals_old.astype(jnp.float32).reshape(seqs, CTX, KV_HEADS, HEAD_DIM)
    old_scores = jnp.einsum('stghd,scgd->sgthc', query_g, keys_c) * scale
    new_scores = jnp.einsum('stghd,sugd->sgthu', query_g, keys_new) * scale
    valid = jnp.arange(CTX, dtype=jnp.int32)[None, :] < lens[:, None]
    old_scores = jnp.where(valid[:, None, None, None, :], old_scores, -1e+30)
    causal = jnp.arange(2)[None, :] <= jnp.arange(2)[:, None]
    new_scores = jnp.where(causal[None, None, :, None, :], new_scores, -1e+30)
    top = jnp.maximum(lax.optimization_barrier(jnp.max(old_scores, axis=-1)), lax.optimization_barrier(jnp.max(new_scores, axis=-1)))
    old_p = jnp.exp(old_scores - top[..., None])
    new_p = jnp.exp(new_scores - top[..., None])
    total = lax.optimization_barrier(jnp.sum(old_p, axis=-1)) + lax.optimization_barrier(jnp.sum(new_p, axis=-1))
    old_w = lax.optimization_barrier(old_p.astype(jnp.bfloat16)).astype(jnp.float32)
    new_w = lax.optimization_barrier(new_p.astype(jnp.bfloat16)).astype(jnp.float32)
    summed = jnp.einsum('sgthc,scgd->stghd', old_w, vals_c) + jnp.einsum('sgthu,sugd->stghd', new_w, vals_new)
    result = summed / jnp.transpose(total, (0, 2, 1, 3))[..., None]
    return result.astype(jnp.bfloat16).reshape(seqs, 2, HEADS * HEAD_DIM)

def reference(token_ids, lengths, embedding, norm_gain, qkv_weight, out_weight, key_cache, value_cache):
    flat_ids = token_ids.reshape(-1).astype(jnp.int32)
    embedded = jnp.take(embedding, flat_ids, axis=0)
    wide = embedded.astype(jnp.float32)
    power = lax.optimization_barrier(jnp.sum(wide * wide, axis=1))
    scaled = (wide * norm_gain[None, :]).astype(jnp.bfloat16)
    summed = jnp.dot(scaled, qkv_weight, preferred_element_type=jnp.float32)
    qkv = (summed * lax.rsqrt(power / D + EPS)[:, None]).astype(jnp.bfloat16)
    kv_width = KV_HEADS * HEAD_DIM
    query = qkv[:, :D].astype(jnp.float32).reshape(BATCH, 2, HEADS, HEAD_DIM)
    keys = qkv[:, D:D + kv_width].astype(jnp.float32).reshape(BATCH, 2, KV_HEADS, HEAD_DIM)
    vals = qkv[:, D + kv_width:].reshape(BATCH, 2, KV_HEADS, HEAD_DIM)
    positions = lengths.astype(jnp.float32)[:, None] + jnp.arange(2, dtype=jnp.float32)[None, :]
    query_r = rotate(query, positions).astype(jnp.bfloat16)
    keys_r = rotate(keys, positions).astype(jnp.bfloat16)
    query_f = lax.optimization_barrier(query_r).astype(jnp.float32)
    keys_f = lax.optimization_barrier(keys_r).astype(jnp.float32)
    vals_f = vals.astype(jnp.float32)
    groups = BATCH // SEQ_DEV

    def split(arr):
        return arr.reshape((groups, SEQ_DEV) + arr.shape[1:])
    attended = lax.map(attend_group, (split(query_f), split(keys_f), split(vals_f), split(key_cache), split(value_cache), split(lengths)))
    attended = attended.reshape(TOKENS, D)
    projected = jnp.dot(attended, out_weight, preferred_element_type=jnp.float32)
    layer_out = (wide + projected).astype(jnp.bfloat16).reshape(BATCH, 2, D)
    new_keys = keys_r.reshape(BATCH, 2, kv_width)
    new_values = vals.reshape(BATCH, 2, kv_width)
    return (layer_out, new_keys, new_values)
```

```python
import jax
import jax.numpy as jnp
from jax import lax
from jax.sharding import PartitionSpec as P

D = 8192
HEADS = 64
KV_HEADS = 8
HEAD_DIM = 128


EPS = 1e-05


def rotate(values, positions):
    half = HEAD_DIM // 2
    freq = jnp.exp(
        -jnp.log(jnp.float32(500000.0)) * 2.0 * jnp.arange(half, dtype=jnp.float32) / HEAD_DIM
    )
    angle = positions[:, :, None, None] * freq[None, None, None, :]
    cosine = jnp.cos(angle)
    sine = jnp.sin(angle)
    lower = values[..., :half]
    upper = values[..., half:]
    return jnp.concatenate([lower * cosine - upper * sine, upper * cosine + lower * sine], axis=-1)


def attend(query, keys_new, vals_new, keys_old, vals_old, lens):
    seqs = query.shape[0]
    slots = keys_old.shape[1]
    group = HEADS // KV_HEADS
    scale = HEAD_DIM ** (-0.5)
    query_g = query.reshape(seqs, 2, KV_HEADS, group, HEAD_DIM)
    keys_c = keys_old.reshape(seqs, slots, KV_HEADS, HEAD_DIM)
    vals_c = vals_old.reshape(seqs, slots, KV_HEADS, HEAD_DIM)
    old_scores = (
        jnp.einsum("stghd,scgd->sgthc", query_g, keys_c, preferred_element_type=jnp.float32) * scale
    )
    new_scores = (
        jnp.einsum("stghd,sugd->sgthu", query_g, keys_new, preferred_element_type=jnp.float32)
        * scale
    )
    valid = jnp.arange(slots, dtype=jnp.int32)[None, :] < lens[:, None]
    old_scores = jnp.where(valid[:, None, None, None, :], old_scores, -1e30)
    causal = jnp.arange(2)[None, :] <= jnp.arange(2)[:, None]
    new_scores = jnp.where(causal[None, None, :, None, :], new_scores, -1e30)
    top = jnp.maximum(jnp.max(old_scores, axis=-1), jnp.max(new_scores, axis=-1))
    old_p = jnp.exp(old_scores - top[..., None])
    new_p = jnp.exp(new_scores - top[..., None])
    total = jnp.sum(old_p, axis=-1) + jnp.sum(new_p, axis=-1)
    summed = jnp.einsum(
        "sgthc,scgd->stghd", old_p.astype(jnp.bfloat16), vals_c, preferred_element_type=jnp.float32
    )
    summed = summed + jnp.einsum(
        "sgthu,sugd->stghd",
        new_p.astype(jnp.bfloat16),
        vals_new,
        preferred_element_type=jnp.float32,
    )
    result = summed / jnp.transpose(total, (0, 2, 1, 3))[..., None]
    return result.astype(jnp.bfloat16).reshape(seqs * 2, HEADS * HEAD_DIM)


def swap(value, axis, flip):
    size = lax.axis_size(axis)
    return lax.ppermute(value, axis, [(i, i ^ flip) for i in range(size)])


def inner_size(size):
    return 2 ** ((size.bit_length() - 1) // 2)


def gather_blocks(block, axis):
    size = lax.axis_size(axis)
    inner = inner_size(size)
    blocks = {0: block}
    for outer in range(size - inner, 0, -inner):
        blocks[outer] = swap(block, axis, outer)
    for outer in range(0, size, inner):
        for flip in range(1, inner):
            blocks[outer + flip] = swap(blocks[outer], axis, flip)
    return [blocks[k] for k in range(size)]


def scatter_sum(parts, axis, inner, wire):
    size = lax.axis_size(axis)
    kept = {}
    for outer in range(size - inner, -1, -inner):
        total = parts[outer]
        for flip in range(1, inner):
            got = swap(parts[outer + flip].astype(wire), axis, flip)
            total = total + got.astype(jnp.float32)
        kept[outer] = total
    total = kept[0]
    for outer in range(inner, size, inner):
        total = total + swap(kept[outer].astype(wire), axis, outer).astype(jnp.float32)
    return total


def token_rows(flat_ids, embedding, order):
    tokens = flat_ids.shape[0]
    span, width = embedding.shape
    size = lax.axis_size("gy")
    me = lax.axis_index("gy")
    room = -(-3 * tokens // (2 * size) // 8) * 8
    owner = flat_ids // span
    at = jnp.arange(tokens, dtype=jnp.int32)
    before = (owner[:, None] == owner[None, :]) & (at[None, :] < at[:, None])
    rank = jnp.sum(before.astype(jnp.int32), axis=1)
    local = jnp.where(owner == me, flat_ids - me * span, 0)
    slot_of = jnp.where(owner == me, rank, -1)
    place = (owner ^ me) * room
    slot = jnp.arange(room, dtype=jnp.int32)
    column = jnp.arange(room * size, dtype=jnp.int32)
    place_o = jnp.take(place, order, axis=0)
    rank_o = jnp.take(rank, order, axis=0)

    def one_round(base):
        mine = (slot_of[None, :] - base) == slot[:, None]
        rows = jnp.sum(jnp.where(mine, local[None, :], 0), axis=1)
        block = jnp.take(embedding, rows, axis=0, mode="clip")
        everything = jnp.concatenate(gather_blocks(block, "gy"), axis=0)
        offset = rank_o - base
        index = jnp.where((offset >= 0) & (offset < room), place_o + offset, -1)
        pick = (index[:, None] == column[None, :]).astype(embedding.dtype)
        return jnp.dot(pick, everything, preferred_element_type=jnp.float32).astype(embedding.dtype)

    most = jnp.max(rank) + 1
    first = one_round(0)

    def more(state):
        return state[0] < most

    def again(state):
        return state[0] + room, state[1] + one_round(state[0])

    return lax.while_loop(more, again, (jnp.int32(room), first))[1]


def on_device(
    token_ids, lengths, embedding, norm_gain, qkv_weight, out_weight, key_cache, value_cache
):
    flat_ids = token_ids.reshape(-1)
    tokens = flat_ids.shape[0]
    gx, gy = lax.axis_size("gx"), lax.axis_size("gy")
    my_x, my_y = lax.axis_index("gx"), lax.axis_index("gy")
    share = tokens // gx
    at = jnp.arange(tokens, dtype=jnp.int32)
    order = ((at // share) ^ my_x) * share + at % share
    features = token_rows(flat_ids, embedding, order)
    wide = features.astype(jnp.float32)
    power = jnp.sum(wide * wide, axis=1)
    scaled = (wide * norm_gain[None, :]).astype(jnp.bfloat16)
    partial = jnp.dot(scaled, qkv_weight, preferred_element_type=jnp.float32)
    my_power = scatter_sum(
        [power[k * share : (k + 1) * share] for k in range(gx)], "gx", 2, jnp.float32
    )
    summed = scatter_sum(
        [partial[k * share : (k + 1) * share] for k in range(gx)], "gx", 2, jnp.bfloat16
    )
    qkv_rows = (summed * lax.rsqrt(my_power / D + EPS)[:, None]).astype(jnp.bfloat16)
    qkv_local = lax.all_to_all(qkv_rows, "gy", split_axis=0, concat_axis=1, tiled=True)
    seqs = lengths.shape[0]
    kv_width = KV_HEADS * HEAD_DIM
    query = qkv_local[:, :D].astype(jnp.float32).reshape(seqs, 2, HEADS, HEAD_DIM)
    keys = qkv_local[:, D : D + kv_width].astype(jnp.float32).reshape(seqs, 2, KV_HEADS, HEAD_DIM)
    vals = qkv_local[:, D + kv_width :].reshape(seqs, 2, KV_HEADS, HEAD_DIM)
    positions = lengths.astype(jnp.float32)[:, None] + jnp.arange(2, dtype=jnp.float32)[None, :]
    query_r = rotate(query, positions).astype(jnp.bfloat16)
    keys_r = rotate(keys, positions).astype(jnp.bfloat16)
    attended = attend(query_r, keys_r, vals, key_cache, value_cache, lengths)
    column_block = lax.all_to_all(attended, "gy", split_axis=1, concat_axis=0, tiled=True)
    lhs = lax.all_gather(column_block, "gx", axis=0, tiled=True)
    mine = tokens // gy
    inner = inner_size(gy)
    outs = [None] * gy
    half = max(gy // 2, inner)
    for low in range(gy - half, -1, -half):
        block = jnp.concatenate(
            [
                lax.dynamic_slice_in_dim(lhs, (my_y ^ k) * mine, mine, 0)
                for k in range(low, low + half)
            ],
            axis=0,
        )
        product = jnp.dot(block, out_weight, preferred_element_type=jnp.float32)
        for k in range(half):
            outs[low + k] = product[k * mine : (k + 1) * mine]
    projected = scatter_sum(outs, "gy", inner, jnp.bfloat16)
    first = my_y * mine
    start = ((first // share) ^ my_x) * share + first % share
    residual = lax.dynamic_slice_in_dim(features, start, mine, 0).astype(jnp.float32)
    layer_out = (
        (residual + projected).astype(jnp.bfloat16).reshape(mine // 2, 2, projected.shape[1])
    )
    new_keys = keys_r.reshape(seqs, 2, kv_width)
    new_values = vals.reshape(seqs, 2, kv_width)
    return (layer_out, new_keys, new_values)


def solution(mesh):
    placed = (
        P(),
        P(("gx", "gy")),
        P("gy", "gx"),
        P("gx"),
        P("gx", "gy"),
        P("gy", "gx"),
        P(("gx", "gy"), None, None),
        P(("gx", "gy"), None, None),
    )
    return jax.shard_map(
        on_device,
        mesh=mesh,
        in_specs=placed,
        out_specs=(P("gy", None, "gx"), P(("gx", "gy"), None, None), P(("gx", "gy"), None, None)),
        check_vma=False,
    )
```
